32 devices in a mesh: dp: 2 (over y), row: 4 (over x, core), col: 4 (over z).
Axes of the slice: x: 2, y: 2, z: 4, core: 2. Of those that a mesh axis runs over, the one named last changes fastest.
Arguments:
- out_grad: float32 [128, 8192], P(('dp', 'row'), 'col'), parts along dimension 0, may hold values from -6 to 6
- hidden: float32 [128, 14336], P(('dp', 'col'), 'row'), parts along dimension 0, may hold values from -0.75 to 0.75
- weight: float32 [14336, 8192], P('row', 'col'), may hold values from -0.046875 to 0.046875
Outputs:
- weight_grad: float32 [28672, 8192], P(('dp', 'row'), 'col'), parts along dimension 0
- hidden_grad: float32 [128, 14336], P(('dp', 'col'), 'row'), parts along dimension 0
The draws below stay inside these ranges and needn't reach their ends.
There are 2 independent parts, one for each index of `dp`. The reference program is written for one: setup_inputs(seed, part) draws one part's arguments, and reference() takes and returns one part's arrays. A program takes and returns all parts, laid end to end along the dimension named above; an argument that names none is the same for every part. Nothing has to cross between parts.
All inputs are finite; a program needn't handle non-finite values.
Results may differ from the reference program's by a relative error of at most 0.000071.
Values sent between devices are 32-bit elements; how exact they have to be, the bound alone decides.
A program may use at most 128 MiB of HBM per device.

```python
import jax
import jax.numpy as jnp
from jax import lax

D = 8192
FF = 14336
TOKENS = 64


def spiked(drawn, rng, source, target, shards_of, factor):
    owner, partner = [(jnp.arange(drawn.shape[axis_at]) // (drawn.shape[axis_at] // shards_of)).reshape([-1 if axis == axis_at else 1 for axis in range(drawn.ndim)]) for axis_at in (source, target)]
    chosen = jax.random.permutation(rng, shards_of)[partner]
    strong = (owner == chosen) | (owner == (partner + shards_of // 2) % shards_of)
    return jnp.where(strong, factor * drawn, drawn)


def shard_levels(own_key, shape, pieces, low, high):
    factor_of, own = 1.0, jax.random.fold_in(own_key, 6)
    for position, parts in pieces:
        heights = jnp.exp(jax.random.uniform(jax.random.fold_in(own, position), (parts,), jnp.float32, low / len(pieces), high / len(pieces)))
        factor_of = factor_of * jnp.repeat(heights, shape[position] // parts).reshape([-1 if axis == position else 1 for axis in range(len(shape))])
    return factor_of


def gaussian(rng, extent, scale, bound, shards=(), dtype=jnp.bfloat16):
    gain = shard_levels(rng, extent, shards, -0.22, 0.18) if shards else 1.0
    result = jax.random.normal(rng, extent, jnp.float32) * scale * gain
    return jnp.minimum(jnp.maximum(result, -bound), bound).astype(dtype)


def gaussian_with(key, shape, scale, reach, shards, heavy, held_as=jnp.bfloat16):
    result = scale * jax.random.normal(key, shape, jnp.float32)
    if shards:
        result = result * shard_levels(key, shape, shards, -0.22, 0.18)
    return jnp.clip(spiked(result, jax.random.fold_in(key, 3), *heavy), -reach, reach).astype(held_as)


def setup_inputs(seed: int = 0, part: int = 0) -> dict:
    key_list = jax.random.split(jax.random.key(seed), 4)
    part_keys = jax.random.split(jax.random.fold_in(key_list[3], part), 4)
    out_grad = gaussian_with(part_keys[0], (TOKENS, D), 1.0, 6.0, ((0, 4), (1, 4)), (1, 0, 4, 2.0), jnp.float32)
    hidden = gaussian(part_keys[1], (TOKENS, FF), TOKENS ** -0.5, 0.75, ((0, 4), (1, 4)), jnp.float32)
    weight = gaussian(key_list[2], (FF, D), FF ** -0.5, 0.046875, ((0, 4), (1, 4)), jnp.float32)
    return {"out_grad": out_grad, "hidden": hidden, "weight": weight}


def reference(out_grad, hidden, weight):
    weight_grad = lax.dot_general(hidden, out_grad, (((0,), (0,)), ((), ())), precision=lax.Precision.HIGHEST, preferred_element_type=jnp.float32)
    hidden_grad = lax.dot_general(out_grad, weight, (((1,), (1,)), ((), ())), precision=lax.Precision.HIGHEST, preferred_element_type=jnp.float32)
    return weight_grad, hidden_grad
```

```python
import functools

import jax
import jax.numpy as jnp
from jax import lax
from jax.experimental import pallas as pl
from jax.experimental.pallas import tpu as pltpu
from jax.sharding import PartitionSpec as P

MESH = pl.DeviceIdType.MESH
LAG = 3
PASSES = 1
EARLY = 3
DELAY = 3
PIECES = 4
HEAD = 2


def split(x):
    high = x.astype(jnp.bfloat16)
    return high, (x - high.astype(jnp.float32)).astype(jnp.bfloat16)


def exchange(
    n_row, n_col, width, g_ref, h_ref, w_ref,
    g_out, h_all, own_out, right_out, left_out,
    g_all, w_buf, part, from_left, from_right,
    w_sem, own_sem, gx_send, gx_recv, gs_send, gs_recv,
    ag_send, ag_recv, rs_send, rs_recv,
):
    t, ff = h_ref.shape
    tg = g_ref.shape[0]
    chunks = ff // width
    tokens = n_row * tg
    chips = n_row // 2
    row, z = lax.axis_index("row"), lax.axis_index("col")
    core = lax.rem(row, 2)
    chip = row // 2
    sibling = row + 1 - 2 * core
    not_first, not_last = z > 0, z < n_col - 1

    barrier = pltpu.get_barrier_semaphore()

    def greet(where):
        pl.semaphore_signal(barrier, inc=1, device_id=where, device_id_type=MESH)

    def peer(k):
        return lax.rem(chip + k, chips) * 2 + core

    for k in range(1, chips):
        greet({"row": peer(k)})
    greet({"row": sibling})

    @pl.when(not_first)
    def _():
        greet({"col": z - 1})

    @pl.when(not_last)
    def _():
        greet({"col": z + 1})

    piece = g_ref.shape[1] // PIECES

    def g_rows(r):
        return g_all.at[pl.ds(pl.multiple_of(r * tg, tg), tg)]

    def part_of(ref, p):
        return ref.at[:, pl.ds(p * piece, piece)]

    own_g = pltpu.make_async_copy(g_ref, g_rows(row), own_sem.at[0])
    mine = pl.ds(pl.multiple_of(z * t, t), t)
    own_h = pltpu.make_async_copy(h_ref, h_all.at[mine], own_sem.at[1])
    own_g.start()
    own_h.start()

    def w_copy(c):
        rows = pl.ds(pl.multiple_of(c * width, width), width)
        return pltpu.make_async_copy(w_ref.at[rows], w_buf.at[rows], w_sem.at[c])

    pl.semaphore_wait(
        barrier, chips + not_first.astype(jnp.int32) + not_last.astype(jnp.int32)
    )

    def across(k, p):
        return pltpu.make_async_remote_copy(
            part_of(g_ref, p), part_of(g_rows(row), p),
            gx_send.at[k - 1, p], gx_recv.at[k - 1, p],
            device_id={"row": peer(k)}, device_id_type=MESH,
        )

    def arrived(k, p):
        source = lax.rem(chip + chips - k, chips) * 2 + core
        view = part_of(g_rows(source), p)
        return pltpu.make_async_remote_copy(
            view, view, gx_send.at[k - 1, p], gx_recv.at[k - 1, p],
            device_id={"row": source}, device_id_type=MESH,
        )

    def aside(k, own, p):
        owner = lax.rem(chip + chips - k, chips) * 2 + (core if own else 1 - core)
        view = part_of(g_rows(owner), p)
        return pltpu.make_async_remote_copy(
            part_of(g_ref, p) if own and k == 0 else view, view,
            gs_send.at[k, p], gs_recv.at[k, p],
            device_id={"row": sibling}, device_id_type=MESH,
        )

    for p in range(PIECES):
        for k in range(1, chips):
            across(k, p).start()
    for p in range(PIECES):
        aside(0, True, p).start()

    def ag(flow, hop, c, shard):
        cols = pl.ds(pl.multiple_of(c * width, width), width)
        rows = pl.ds(pl.multiple_of(shard * t, t), t)
        index = c if hop is None else hop * chunks + c
        view = h_all.at[rows, cols]
        return pltpu.make_async_remote_copy(
            h_ref.at[:, cols] if hop is None else view, view, ag_send.at[flow, index], ag_recv.at[flow, index],
            device_id={"col": z + 1 - 2 * flow}, device_id_type=MESH,
        )

    def going(flow):
        return not_first if flow else not_last

    def first_hop(c, carry):
        for flow in range(2):

            @pl.when(going(flow))
            def _():
                ag(flow, None, c, z).start()

        return carry

    lax.fori_loop(0, chunks, first_hop, 0)
    for c in range(chunks):
        w_copy(c).start()

    def pass_on(hop, c):
        for flow in range(2):
            shard = z + hop if flow else z - hop
            there = (shard < n_col) if flow else (shard >= 0)

            @pl.when(there & going(flow))
            def _():
                ag(flow, hop - 1, c, shard).wait_recv()
                ag(flow, hop, c, shard).start()

    early_items = min(EARLY, chunks)
    rest_each = -(-(chunks - early_items) // PIECES)
    items = (n_col - 3) * chunks

    def early(c, carry):
        pass_on(1, c)
        return carry

    lax.fori_loop(0, early_items, early, 0)
    own_g.wait()
    own_h.wait()
    contract = (((1,), (1,)), ((), ()))

    def partial(at, ks):
        w_high, w_low = split(w_buf[at, ks])
        both = lax.dot_general(
            g_out[pl.ds(0, 2 * tokens), ks], w_high, contract,
            preferred_element_type=jnp.float32,
        )
        rest = lax.dot_general(
            g_out[pl.ds(0, tokens), ks], w_low, contract,
            preferred_element_type=jnp.float32,
        )
        return both[:tokens] + (both[tokens:] + rest)

    def relay(p):
        for k in range(1, chips):
            arrived(k, p).wait_recv()
            aside(k, True, p).start()

    relay(0)
    for p in range(PIECES):
        if p + 1 < PIECES:
            relay(p + 1)
        for k in range(chips):
            aside(k, False, p).wait_recv()
        ks = pl.ds(p * piece, piece)
        high, low = split(g_all[:, ks])
        g_out[pl.ds(0, tokens), ks] = high
        g_out[pl.ds(tokens, tokens), ks] = low
        g_out[pl.ds(2 * tokens, tokens), ks] = high
        for c in range(HEAD):
            at = pl.ds(c * width, width)
            if p == 0:
                w_copy(c).wait()
                part[:, at] = partial(at, ks)
            else:
                part[:, at] += partial(at, ks)
        at = early_items + p * rest_each
        lax.fori_loop(at, min(at + rest_each, chunks), early, 0)

    def rs(flow, d, c, source):
        held = from_right if flow else from_left
        at = pl.ds(d * t, t), pl.ds(pl.multiple_of(c * width, width), width)
        index = d * chunks + c
        return pltpu.make_async_remote_copy(
            source.at[at], held.at[at], rs_send.at[flow, index],
            rs_recv.at[flow, index],
            device_id={"col": z + 1 - 2 * flow}, device_id_type=MESH,
        )

    def sums(flow, c):
        held = from_right if flow else from_left
        out = left_out if flow else right_out
        cols = pl.ds(pl.multiple_of(c * width, width), width)
        first = (z == n_col - 1) if flow else (z == 0)
        for d in range(n_col - 1) if flow else range(n_col - 1, 0, -1):
            rows = pl.ds(d * t, t)
            on = (d < z) if flow else (d > z)
            near = (d == z - 1) if flow else (d == z + 1)

            @pl.when(on & jnp.logical_not(first))
            def _():
                rs(flow, d, c, held).wait_recv()

            @pl.when(near & first)
            def _():
                out[:, cols] = part[rows, cols]

            @pl.when(near & jnp.logical_not(first))
            def _():
                out[:, cols] = held[rows, cols] + part[rows, cols]

            far = on & jnp.logical_not(near)

            @pl.when(far & first)
            def _():
                rs(flow, d, c, part).start()

            @pl.when(far & jnp.logical_not(first))
            def _():
                held[rows, cols] += part[rows, cols]
                rs(flow, d, c, held).start()

    steps = max(chunks + LAG * (n_col - 2), -(-items // PASSES) + DELAY)

    def step(i, carry):
        @pl.when((i >= HEAD) & (i < chunks))
        def _():
            w_copy(i).wait()
            at = pl.ds(pl.multiple_of(i * width, width), width)
            part[:, at] = partial(at, pl.ds(0, g_ref.shape[1]))

        for flow in range(2):
            c = i - LAG * (n_col - 1 - z if flow else z)

            @pl.when((c >= 0) & (c < chunks))
            def _():
                sums(flow, c)

        for k in range(PASSES):
            item = PASSES * (i - DELAY) + k

            @pl.when((item >= 0) & (item < items))
            def _():
                hop, c = item // chunks + 2, lax.rem(item, chunks)
                pass_on(hop, c)

        return carry

    lax.fori_loop(0, steps, step, 0)

    own_out[...] = part[mine]

    def finish(c, carry):
        for flow in range(2):
            for hop in range(1, n_col):
                shard = z + hop if flow else z - hop
                there = (shard < n_col) if flow else (shard >= 0)

                @pl.when(there & jnp.logical_not(going(flow)))
                def _():
                    ag(flow, hop - 1, c, shard).wait_recv()

        return carry

    lax.fori_loop(0, chunks, finish, 0)

    for p in range(PIECES):
        for k in range(1, chips):
            across(k, p).wait_send()
        for k in range(chips):
            aside(k, True, p).wait_send()

    def drain(c, carry):
        for flow in range(2):
            @pl.when(going(flow))
            def _():
                ag(flow, None, c, z).wait_send()

            for hop in range(1, n_col - 1):
                shard = z + hop if flow else z - hop
                there = (shard < n_col) if flow else (shard >= 0)

                @pl.when(there & going(flow))
                def _():
                    ag(flow, hop, c, shard).wait_send()

            for d in range(n_col):

                @pl.when((d < z - 1) if flow else (d > z + 1))
                def _():
                    rs(flow, d, c, part).wait_send()

        return carry

    lax.fori_loop(0, chunks, drain, 0)


def outer(tile, h_ref, g_ref, out_ref, buf, out_sem):
    ff = h_ref.shape[1]

    def give(i):
        at = pl.ds(i * tile, tile)
        return pltpu.make_async_copy(buf.at[at], out_ref.at[at], out_sem.at[i])

    for i in range(ff // tile):
        at = pl.ds(i * tile, tile)
        high, low = split(h_ref[:, at])
        buf[at] = lax.dot_general(
            jnp.concatenate([high, high, low], axis=0), g_ref[...],
            (((0,), (0,)), ((), ())), preferred_element_type=jnp.float32,
        )
        give(i).start()
    for i in range(ff // tile):
        give(i).wait()


def on_device(n_row, n_col, out_grad, hidden, weight):
    f32, bf16 = jnp.float32, jnp.bfloat16
    (tg, d), (t, ff) = out_grad.shape, hidden.shape
    tokens = n_row * tg
    dma = pltpu.SemaphoreType.DMA
    whole = pl.BlockSpec(memory_space=pltpu.VMEM)
    anywhere = pl.BlockSpec(memory_space=pltpu.HBM)
    chips = n_row // 2
    wide = ff % 256 == 0 and ff > 1024
    width = 512 if wide else 128
    chunks = ff // width
    g_parts, h_all, own, right, left = pl.pallas_call(
        functools.partial(exchange, n_row, n_col, width),
        out_shape=(
            pltpu.VMEM((3 * tokens, d), bf16),
            pltpu.VMEM((tokens, ff), f32),
            jax.ShapeDtypeStruct((t, ff), f32),
            jax.ShapeDtypeStruct((t, ff), f32),
            jax.ShapeDtypeStruct((t, ff), f32),
        ),
        in_specs=[anywhere] * 3,
        out_specs=(whole,) * 5,
        scratch_shapes=[
            pltpu.VMEM((tokens, d), f32),
            pltpu.VMEM((ff, d), f32),
            pltpu.VMEM((tokens, ff), f32),
            pltpu.VMEM((tokens, ff), f32),
            pltpu.VMEM((tokens, ff), f32),
            dma((chunks,)),
            dma((2,)),
            dma((max(chips - 1, 1), PIECES)),
            dma((max(chips - 1, 1), PIECES)),
            dma((chips, PIECES)),
            dma((chips, PIECES)),
            dma((2, (n_col - 1) * chunks)),
            dma((2, (n_col - 1) * chunks)),
            dma((2, n_col * chunks)),
            dma((2, n_col * chunks)),
        ],
        compiler_params=pltpu.CompilerParams(
            collective_id=0, has_side_effects=True, vmem_limit_bytes=48 << 20
        ),
        name="exchange",
    )(*(pltpu.with_memory_space_constraint(x, pltpu.HBM) for x in (out_grad, hidden, weight)))
    from_left = lax.ppermute(right, "col", [(z, z + 1) for z in range(n_col - 1)])
    from_right = lax.ppermute(left, "col", [(z + 1, z) for z in range(n_col - 1)])
    tile = 256 if wide else 128
    weight_grad = pl.pallas_call(
        functools.partial(outer, tile),
        out_shape=jax.ShapeDtypeStruct((ff, d), f32),
        in_specs=[whole] * 2,
        out_specs=anywhere,
        scratch_shapes=[
            pltpu.VMEM((ff, d), f32),
            dma((ff // tile,)),
        ],
        compiler_params=pltpu.CompilerParams(vmem_limit_bytes=48 << 20),
        cost_estimate=pl.CostEstimate(
            flops=6 * tokens * ff * d, bytes_accessed=4 * ff * d, transcendentals=0
        ),
        name="outer",
    )(h_all, g_parts)
    return weight_grad, own + (from_left + from_right)


def solution(mesh):
    placed = (P(("dp", "row"), "col"), P(("dp", "col"), "row"), P("row", "col"))
    return jax.shard_map(
        functools.partial(on_device, mesh.shape["row"], mesh.shape["col"]),
        mesh=mesh,
        in_specs=placed,
        out_specs=(P(("dp", "row"), "col"), P(("dp", "col"), "row")),
        check_vma=False,
    )
```

```python
import functools

import jax
import jax.numpy as jnp
from jax import lax
from jax.experimental import pallas as pl
from jax.experimental.pallas import tpu as pltpu
from jax.sharding import PartitionSpec as P

MESH = pl.DeviceIdType.MESH
LAG = 3
PASSES = 2
EARLY = 3
DELAY = 3
PIECES = 4
HEAD = 2


def split(x):
    high = x.astype(jnp.bfloat16)
    return high, (x - high.astype(jnp.float32)).astype(jnp.bfloat16)


def exchange(
    n_row, n_col, width, g_ref, h_ref, w_ref,
    g_out, h_all, own_out, right_out, left_out,
    g_all, w_buf, part, from_left, from_right,
    w_sem, own_sem, gx_send, gx_recv, gs_send, gs_recv,
    ag_send, ag_recv, rs_send, rs_recv,
):
    t, ff = h_ref.shape
    tg = g_ref.shape[0]
    chunks = ff // width
    tokens = n_row * tg
    chips = n_row // 2
    row, z = lax.axis_index("row"), lax.axis_index("col")
    core = lax.rem(row, 2)
    chip = row // 2
    sibling = row + 1 - 2 * core
    not_first, not_last = z > 0, z < n_col - 1

    barrier = pltpu.get_barrier_semaphore()

    def greet(where):
        pl.semaphore_signal(barrier, inc=1, device_id=where, device_id_type=MESH)

    def peer(k):
        return lax.rem(chip + k, chips) * 2 + core

    for k in range(1, chips):
        greet({"row": peer(k)})
    greet({"row": sibling})

    @pl.when(not_first)
    def _():
        greet({"col": z - 1})

    @pl.when(not_last)
    def _():
        greet({"col": z + 1})

    piece = g_ref.shape[1] // PIECES

    def g_rows(r):
        return g_all.at[pl.ds(pl.multiple_of(r * tg, tg), tg)]

    def part_of(ref, p):
        return ref.at[:, pl.ds(p * piece, piece)]

    own_g = pltpu.make_async_copy(g_ref, g_rows(row), own_sem.at[0])
    mine = pl.ds(pl.multiple_of(z * t, t), t)
    own_h = pltpu.make_async_copy(h_ref, h_all.at[mine], own_sem.at[1])
    own_g.start()
    own_h.start()

    def w_copy(c):
        rows = pl.ds(pl.multiple_of(c * width, width), width)
        return pltpu.make_async_copy(w_ref.at[rows], w_buf.at[rows], w_sem.at[c])

    pl.semaphore_wait(
        barrier, chips + not_first.astype(jnp.int32) + not_last.astype(jnp.int32)
    )

    def across(k, p):
        return pltpu.make_async_remote_copy(
            part_of(g_ref, p), part_of(g_rows(row), p),
            gx_send.at[k - 1, p], gx_recv.at[k - 1, p],
            device_id={"row": peer(k)}, device_id_type=MESH,
        )

    def arrived(k, p):
        source = lax.rem(chip + chips - k, chips) * 2 + core
        view = part_of(g_rows(source), p)
        return pltpu.make_async_remote_copy(
            view, view, gx_send.at[k - 1, p], gx_recv.at[k - 1, p],
            device_id={"row": source}, device_id_type=MESH,
        )

    def aside(k, own, p):
        owner = lax.rem(chip + chips - k, chips) * 2 + (core if own else 1 - core)
        view = part_of(g_rows(owner), p)
        return pltpu.make_async_remote_copy(
            part_of(g_ref, p) if own and k == 0 else view, view,
            gs_send.at[k, p], gs_recv.at[k, p],
            device_id={"row": sibling}, device_id_type=MESH,
        )

    for p in range(PIECES):
        for k in range(1, chips):
            across(k, p).start()
    for p in range(PIECES):
        aside(0, True, p).start()

    def ag(flow, hop, c, shard):
        cols = pl.ds(pl.multiple_of(c * width, width), width)
        rows = pl.ds(pl.multiple_of(shard * t, t), t)
        index = c if hop is None else hop * chunks + c
        view = h_all.at[rows, cols]
        return pltpu.make_async_remote_copy(
            h_ref.at[:, cols] if hop is None else view, view, ag_send.at[flow, index], ag_recv.at[flow, index],
            device_id={"col": z + 1 - 2 * flow}, device_id_type=MESH,
        )

    def going(flow):
        return not_first if flow else not_last

    def first_hop(c, carry):
        for flow in range(2):

            @pl.when(going(flow))
            def _():
                ag(flow, None, c, z).start()

        return carry

    lax.fori_loop(0, chunks, first_hop, 0)
    for c in range(chunks):
        w_copy(c).start()

    def pass_on(hop, c):
        for flow in range(2):
            shard = z + hop if flow else z - hop
            there = (shard < n_col) if flow else (shard >= 0)

            @pl.when(there & going(flow))
            def _():
                ag(flow, hop - 1, c, shard).wait_recv()
                ag(flow, hop, c, shard).start()

    early_items = min(EARLY, chunks)
    rest_each = -(-(chunks - early_items) // PIECES)
    items = (n_col - 3) * chunks

    def early(c, carry):
        pass_on(1, c)
        return carry

    lax.fori_loop(0, early_items, early, 0)
    own_g.wait()
    own_h.wait()
    contract = (((1,), (1,)), ((), ()))

    def partial(at, ks):
        w_high, w_low = split(w_buf[at, ks])
        both = lax.dot_general(
            g_out[pl.ds(0, 2 * tokens), ks], w_high, contract,
            preferred_element_type=jnp.float32,
        )
        rest = lax.dot_general(
            g_out[pl.ds(0, tokens), ks], w_low, contract,
            preferred_element_type=jnp.float32,
        )
        return both[:tokens] + (both[tokens:] + rest)

    def relay(p):
        for k in range(1, chips):
            arrived(k, p).wait_recv()
            aside(k, True, p).start()

    relay(0)
    for p in range(PIECES):
        if p + 1 < PIECES:
            relay(p + 1)
        for k in range(chips):
            aside(k, False, p).wait_recv()
        ks = pl.ds(p * piece, piece)
        high, low = split(g_all[:, ks])
        g_out[pl.ds(0, tokens), ks] = high
        g_out[pl.ds(tokens, tokens), ks] = low
        g_out[pl.ds(2 * tokens, tokens), ks] = high
        for c in range(HEAD):
            at = pl.ds(c * width, width)
            if p == 0:
                w_copy(c).wait()
                part[:, at] = partial(at, ks)
            else:
                part[:, at] += partial(at, ks)
        at = early_items + p * rest_each
        lax.fori_loop(at, min(at + rest_each, chunks), early, 0)

    def rs(flow, d, c, source):
        held = from_right if flow else from_left
        at = pl.ds(d * t, t), pl.ds(pl.multiple_of(c * width, width), width)
        index = d * chunks + c
        return pltpu.make_async_remote_copy(
            source.at[at], held.at[at], rs_send.at[flow, index],
            rs_recv.at[flow, index],
            device_id={"col": z + 1 - 2 * flow}, device_id_type=MESH,
        )

    def sums(flow, d, c):
        held = from_right if flow else from_left
        out = left_out if flow else right_out
        cols = pl.ds(pl.multiple_of(c * width, width), width)
        rows = pl.ds(d * t, t)
        first = (z == n_col - 1) if flow else (z == 0)
        near = (d == z - 1) if flow else (d == z + 1)

        @pl.when(jnp.logical_not(first))
        def _():
            rs(flow, d, c, held).wait_recv()

        @pl.when(near & first)
        def _():
            out[:, cols] = part[rows, cols]

        @pl.when(near & jnp.logical_not(first))
        def _():
            out[:, cols] = held[rows, cols] + part[rows, cols]

        far = jnp.logical_not(near)

        @pl.when(far & first)
        def _():
            rs(flow, d, c, part).start()

        @pl.when(far & jnp.logical_not(first))
        def _():
            held[rows, cols] += part[rows, cols]
            rs(flow, d, c, held).start()

    steps = max(chunks + LAG * (n_col - 2), -(-items // PASSES) + DELAY)

    def step(i, carry):
        @pl.when((i >= HEAD) & (i < chunks))
        def _():
            w_copy(i).wait()
            at = pl.ds(pl.multiple_of(i * width, width), width)
            part[:, at] = partial(at, pl.ds(0, g_ref.shape[1]))

        for flow in range(2):
            for d in range(n_col - 1) if flow else range(n_col - 1, 0, -1):
                c = i - LAG * (n_col - 1 - z if flow else z)
                c -= d if flow else n_col - 1 - d
                on = (d < z) if flow else (d > z)

                @pl.when(on & (c >= 0) & (c < chunks))
                def _():
                    sums(flow, d, c)

        for k in range(PASSES):
            item = PASSES * (i - DELAY) + k

            @pl.when((item >= 0) & (item < items))
            def _():
                hop, c = item // chunks + 2, lax.rem(item, chunks)
                pass_on(hop, c)

        return carry

    lax.fori_loop(0, steps, step, 0)

    own_out[...] = part[mine]

    def finish(c, carry):
        for flow in range(2):
            for hop in range(1, n_col):
                shard = z + hop if flow else z - hop
                there = (shard < n_col) if flow else (shard >= 0)

                @pl.when(there & jnp.logical_not(going(flow)))
                def _():
                    ag(flow, hop - 1, c, shard).wait_recv()

        return carry

    lax.fori_loop(0, chunks, finish, 0)

    for p in range(PIECES):
        for k in range(1, chips):
            across(k, p).wait_send()
        for k in range(chips):
            aside(k, True, p).wait_send()

    def drain(c, carry):
        for flow in range(2):
            @pl.when(going(flow))
            def _():
                ag(flow, None, c, z).wait_send()

            for hop in range(1, n_col - 1):
                shard = z + hop if flow else z - hop
                there = (shard < n_col) if flow else (shard >= 0)

                @pl.when(there & going(flow))
                def _():
                    ag(flow, hop, c, shard).wait_send()

            for d in range(n_col):

                @pl.when((d < z - 1) if flow else (d > z + 1))
                def _():
                    rs(flow, d, c, part).wait_send()

        return carry

    lax.fori_loop(0, chunks, drain, 0)


def outer(tile, h_ref, g_ref, out_ref, buf, out_sem):
    ff = h_ref.shape[1]

    def give(i):
        at = pl.ds(i * tile, tile)
        return pltpu.make_async_copy(buf.at[at], out_ref.at[at], out_sem.at[i])

    for i in range(ff // tile):
        at = pl.ds(i * tile, tile)
        high, low = split(h_ref[:, at])
        buf[at] = lax.dot_general(
            jnp.concatenate([high, high, low], axis=0), g_ref[...],
            (((0,), (0,)), ((), ())), preferred_element_type=jnp.float32,
        )
        give(i).start()
    for i in range(ff // tile):
        give(i).wait()


def on_device(n_row, n_col, out_grad, hidden, weight):
    f32, bf16 = jnp.float32, jnp.bfloat16
    (tg, d), (t, ff) = out_grad.shape, hidden.shape
    tokens = n_row * tg
    dma = pltpu.SemaphoreType.DMA
    whole = pl.BlockSpec(memory_space=pltpu.VMEM)
    anywhere = pl.BlockSpec(memory_space=pltpu.HBM)
    chips = n_row // 2
    wide = ff % 256 == 0 and ff > 1024
    width = 512 if wide else 128
    chunks = ff // width
    g_parts, h_all, own, right, left = pl.pallas_call(
        functools.partial(exchange, n_row, n_col, width),
        out_shape=(
            pltpu.VMEM((3 * tokens, d), bf16),
            pltpu.VMEM((tokens, ff), f32),
            jax.ShapeDtypeStruct((t, ff), f32),
            jax.ShapeDtypeStruct((t, ff), f32),
            jax.ShapeDtypeStruct((t, ff), f32),
        ),
        in_specs=[anywhere] * 3,
        out_specs=(whole,) * 5,
        scratch_shapes=[
            pltpu.VMEM((tokens, d), f32),
            pltpu.VMEM((ff, d), f32),
            pltpu.VMEM((tokens, ff), f32),
            pltpu.VMEM((tokens, ff), f32),
            pltpu.VMEM((tokens, ff), f32),
            dma((chunks,)),
            dma((2,)),
            dma((max(chips - 1, 1), PIECES)),
            dma((max(chips - 1, 1), PIECES)),
            dma((chips, PIECES)),
            dma((chips, PIECES)),
            dma((2, (n_col - 1) * chunks)),
            dma((2, (n_col - 1) * chunks)),
            dma((2, n_col * chunks)),
            dma((2, n_col * chunks)),
        ],
        compiler_params=pltpu.CompilerParams(
            collective_id=0, has_side_effects=True, vmem_limit_bytes=48 << 20
        ),
        name="exchange",
    )(*(pltpu.with_memory_space_constraint(x, pltpu.HBM) for x in (out_grad, hidden, weight)))
    from_left = lax.ppermute(right, "col", [(z, z + 1) for z in range(n_col - 1)])
    from_right = lax.ppermute(left, "col", [(z + 1, z) for z in range(n_col - 1)])
    tile = 256 if wide else 128
    weight_grad = pl.pallas_call(
        functools.partial(outer, tile),
        out_shape=jax.ShapeDtypeStruct((ff, d), f32),
        in_specs=[whole] * 2,
        out_specs=anywhere,
        scratch_shapes=[
            pltpu.VMEM((ff, d), f32),
            dma((ff // tile,)),
        ],
        compiler_params=pltpu.CompilerParams(vmem_limit_bytes=48 << 20),
        cost_estimate=pl.CostEstimate(
            flops=6 * tokens * ff * d, bytes_accessed=4 * ff * d, transcendentals=0
        ),
        name="outer",
    )(h_all, g_parts)
    return weight_grad, own + (from_left + from_right)


def solution(mesh):
    placed = (P(("dp", "row"), "col"), P(("dp", "col"), "row"), P("row", "col"))
    return jax.shard_map(
        functools.partial(on_device, mesh.shape["row"], mesh.shape["col"]),
        mesh=mesh,
        in_specs=placed,
        out_specs=(P(("dp", "row"), "col"), P(("dp", "col"), "row")),
        check_vma=False,
    )
```

```python
import functools

import jax
import jax.numpy as jnp
from jax import lax
from jax.experimental import pallas as pl
from jax.experimental.pallas import tpu as pltpu
from jax.sharding import PartitionSpec as P

MESH = pl.DeviceIdType.MESH
LAG = 2
PASSES = 2
EARLY = 2


def split(x):
    high = x.astype(jnp.bfloat16)
    return high, (x - high.astype(jnp.float32)).astype(jnp.bfloat16)


def exchange(
    n_row, n_col, width, g_ref, h_ref, w_ref,
    g_out, h_out, own_out, right_out, left_out,
    g_all, h_all, w_buf, part, from_left, from_right,
    w_sem, own_sem, gx_send, gx_recv, gs_send, gs_recv,
    ag_send, ag_recv, rs_send, rs_recv,
):
    t, ff = h_ref.shape
    tg = g_ref.shape[0]
    chunks = ff // width
    tokens = n_row * tg
    chips = n_row // 2
    row, z = lax.axis_index("row"), lax.axis_index("col")
    core = lax.rem(row, 2)
    chip = row // 2
    sibling = row + 1 - 2 * core
    not_first, not_last = z > 0, z < n_col - 1

    barrier = pltpu.get_barrier_semaphore()

    def greet(where):
        pl.semaphore_signal(barrier, inc=1, device_id=where, device_id_type=MESH)

    def peer(k):
        return lax.rem(chip + k, chips) * 2 + core

    for k in range(1, chips):
        greet({"row": peer(k)})
    greet({"row": sibling})

    @pl.when(not_first)
    def _():
        greet({"col": z - 1})

    @pl.when(not_last)
    def _():
        greet({"col": z + 1})

    def g_rows(r):
        return g_all.at[pl.ds(pl.multiple_of(r * tg, tg), tg)]

    own_g = pltpu.make_async_copy(g_ref, g_rows(row), own_sem.at[0])
    mine = pl.ds(pl.multiple_of(z * t, t), t)
    own_h = pltpu.make_async_copy(h_ref, h_all.at[mine], own_sem.at[1])
    own_g.start()
    own_h.start()

    def w_copy(c):
        rows = pl.ds(pl.multiple_of(c * width, width), width)
        return pltpu.make_async_copy(w_ref.at[rows], w_buf.at[rows], w_sem.at[c])

    pl.semaphore_wait(
        barrier, chips + not_first.astype(jnp.int32) + not_last.astype(jnp.int32)
    )

    def across(k):
        return pltpu.make_async_remote_copy(
            g_ref, g_rows(row), gx_send.at[k - 1], gx_recv.at[k - 1],
            device_id={"row": peer(k)}, device_id_type=MESH,
        )

    def arrived(k):
        source = lax.rem(chip + chips - k, chips) * 2 + core
        return pltpu.make_async_remote_copy(
            g_rows(source), g_rows(source), gx_send.at[k - 1], gx_recv.at[k - 1],
            device_id={"row": source}, device_id_type=MESH,
        )

    def aside(k, own):
        owner = lax.rem(chip + chips - k, chips) * 2 + (core if own else 1 - core)
        return pltpu.make_async_remote_copy(
            g_ref if own and k == 0 else g_rows(owner), g_rows(owner), gs_send.at[k], gs_recv.at[k],
            device_id={"row": sibling}, device_id_type=MESH,
        )

    for k in range(1, chips):
        across(k).start()
    aside(0, True).start()

    def ag(flow, hop, c, shard):
        cols = pl.ds(pl.multiple_of(c * width, width), width)
        rows = pl.ds(pl.multiple_of(shard * t, t), t)
        index = c if hop is None else hop * chunks + c
        view = h_all.at[rows, cols]
        return pltpu.make_async_remote_copy(
            h_ref.at[:, cols] if hop is None else view, view, ag_send.at[flow, index], ag_recv.at[flow, index],
            device_id={"col": z + 1 - 2 * flow}, device_id_type=MESH,
        )

    def going(flow):
        return not_first if flow else not_last

    def first_hop(c, carry):
        for flow in range(2):

            @pl.when(going(flow))
            def _():
                ag(flow, None, c, z).start()

        return carry

    lax.fori_loop(0, chunks, first_hop, 0)
    for c in range(chunks):
        w_copy(c).start()

    def pass_on(hop, c):
        for flow in range(2):
            shard = z + hop if flow else z - hop
            there = (shard < n_col) if flow else (shard >= 0)

            @pl.when(there & going(flow))
            def _():
                ag(flow, hop - 1, c, shard).wait_recv()
                ag(flow, hop, c, shard).start()

    items = (n_col - 2) * chunks

    def early(c, carry):
        pass_on(1, c)
        return carry

    lax.fori_loop(0, EARLY, early, 0)
    for k in range(1, chips):
        arrived(k).wait_recv()
        aside(k, True).start()
    for k in range(chips):
        aside(k, False).wait_recv()
    own_g.wait()
    own_h.wait()
    high, low = split(g_all[...])
    g_out[pl.ds(0, tokens)] = high
    g_out[pl.ds(tokens, tokens)] = low
    g_out[pl.ds(2 * tokens, tokens)] = high

    def rs(flow, d, c, source):
        held = from_right if flow else from_left
        at = pl.ds(d * t, t), pl.ds(pl.multiple_of(c * width, width), width)
        index = d * chunks + c
        return pltpu.make_async_remote_copy(
            source.at[at], held.at[at], rs_send.at[flow, index],
            rs_recv.at[flow, index],
            device_id={"col": z + 1 - 2 * flow}, device_id_type=MESH,
        )

    def sums(flow, c):
        held = from_right if flow else from_left
        out = left_out if flow else right_out
        cols = pl.ds(pl.multiple_of(c * width, width), width)
        first = (z == n_col - 1) if flow else (z == 0)
        for d in range(n_col - 1) if flow else range(n_col - 1, 0, -1):
            rows = pl.ds(d * t, t)
            on = (d < z) if flow else (d > z)
            near = (d == z - 1) if flow else (d == z + 1)

            @pl.when(on & jnp.logical_not(first))
            def _():
                rs(flow, d, c, held).wait_recv()

            @pl.when(near & first)
            def _():
                out[:, cols] = part[rows, cols]

            @pl.when(near & jnp.logical_not(first))
            def _():
                out[:, cols] = held[rows, cols] + part[rows, cols]

            far = on & jnp.logical_not(near)

            @pl.when(far & first)
            def _():
                rs(flow, d, c, part).start()

            @pl.when(far & jnp.logical_not(first))
            def _():
                held[rows, cols] += part[rows, cols]
                rs(flow, d, c, held).start()

    contract = (((1,), (1,)), ((), ()))
    steps = max(chunks + LAG * (n_col - 2), -(-(items - EARLY) // PASSES))

    def step(i, carry):
        @pl.when(i < chunks)
        def _():
            c = i
            w_copy(c).wait()
            at = pl.ds(pl.multiple_of(c * width, width), width)
            w_high, w_low = split(w_buf[at, :])
            both = lax.dot_general(
                g_out[pl.ds(0, 2 * tokens)], w_high, contract,
                preferred_element_type=jnp.float32,
            )
            rest = lax.dot_general(
                g_out[pl.ds(0, tokens)], w_low, contract,
                preferred_element_type=jnp.float32,
            )
            part[:, at] = both[:tokens] + (both[tokens:] + rest)

        for flow in range(2):
            c = i - LAG * (n_col - 1 - z if flow else z)

            @pl.when((c >= 0) & (c < chunks))
            def _():
                sums(flow, c)

        for k in range(PASSES):
            item = EARLY + PASSES * i + k

            @pl.when(item < items)
            def _():
                hop, c = item // chunks + 1, lax.rem(item, chunks)
                pass_on(hop, c)

        return carry

    lax.fori_loop(0, steps, step, 0)

    own_out[...] = part[mine]

    def finish(c, carry):
        for flow in range(2):
            for hop in range(1, n_col):
                shard = z + hop if flow else z - hop
                there = (shard < n_col) if flow else (shard >= 0)

                @pl.when(there & jnp.logical_not(going(flow)))
                def _():
                    ag(flow, hop - 1, c, shard).wait_recv()

        at = pl.ds(pl.multiple_of(c * width, width), width)
        high, low = split(h_all[:, at])
        h_out[pl.ds(0, tokens), at] = high
        h_out[pl.ds(tokens, tokens), at] = high
        h_out[pl.ds(2 * tokens, tokens), at] = low
        return carry

    lax.fori_loop(0, chunks, finish, 0)

    for k in range(1, chips):
        across(k).wait_send()
    for k in range(chips):
        aside(k, True).wait_send()

    def drain(c, carry):
        for flow in range(2):
            @pl.when(going(flow))
            def _():
                ag(flow, None, c, z).wait_send()

            for hop in range(1, n_col - 1):
                shard = z + hop if flow else z - hop
                there = (shard < n_col) if flow else (shard >= 0)

                @pl.when(there & going(flow))
                def _():
                    ag(flow, hop, c, shard).wait_send()

            for d in range(n_col):

                @pl.when((d < z - 1) if flow else (d > z + 1))
                def _():
                    rs(flow, d, c, part).wait_send()

        return carry

    lax.fori_loop(0, chunks, drain, 0)


def outer(tile, h_ref, g_ref, out_ref, buf, out_sem):
    ff = h_ref.shape[1]

    def give(i):
        at = pl.ds(i * tile, tile)
        return pltpu.make_async_copy(buf.at[at], out_ref.at[at], out_sem.at[i])

    for i in range(ff // tile):
        at = pl.ds(i * tile, tile)
        buf[at] = lax.dot_general(
            h_ref[:, at], g_ref[...],
            (((0,), (0,)), ((), ())), preferred_element_type=jnp.float32,
        )
        give(i).start()
    for i in range(ff // tile):
        give(i).wait()


def on_device(n_row, n_col, out_grad, hidden, weight):
    f32, bf16 = jnp.float32, jnp.bfloat16
    (tg, d), (t, ff) = out_grad.shape, hidden.shape
    tokens = n_row * tg
    dma = pltpu.SemaphoreType.DMA
    whole = pl.BlockSpec(memory_space=pltpu.VMEM)
    anywhere = pl.BlockSpec(memory_space=pltpu.HBM)
    chips = n_row // 2
    wide = ff % 256 == 0 and ff > 1024
    width = 512 if wide else 128
    chunks = ff // width
    g_parts, h_parts, own, right, left = pl.pallas_call(
        functools.partial(exchange, n_row, n_col, width),
        out_shape=(
            pltpu.VMEM((3 * tokens, d), bf16),
            pltpu.VMEM((3 * tokens, ff), bf16),
            jax.ShapeDtypeStruct((t, ff), f32),
            jax.ShapeDtypeStruct((t, ff), f32),
            jax.ShapeDtypeStruct((t, ff), f32),
        ),
        in_specs=[anywhere] * 3,
        out_specs=(whole,) * 5,
        scratch_shapes=[
            pltpu.VMEM((tokens, d), f32),
            pltpu.VMEM((tokens, ff), f32),
            pltpu.VMEM((ff, d), f32),
            pltpu.VMEM((tokens, ff), f32),
            pltpu.VMEM((tokens, ff), f32),
            pltpu.VMEM((tokens, ff), f32),
            dma((chunks,)),
            dma((2,)),
            dma((max(chips - 1, 1),)),
            dma((max(chips - 1, 1),)),
            dma((chips,)),
            dma((chips,)),
            dma((2, (n_col - 1) * chunks)),
            dma((2, (n_col - 1) * chunks)),
            dma((2, n_col * chunks)),
            dma((2, n_col * chunks)),
        ],
        compiler_params=pltpu.CompilerParams(
            collective_id=0, has_side_effects=True, vmem_limit_bytes=48 << 20
        ),
        name="exchange",
    )(*(pltpu.with_memory_space_constraint(x, pltpu.HBM) for x in (out_grad, hidden, weight)))
    from_left = lax.ppermute(right, "col", [(z, z + 1) for z in range(n_col - 1)])
    from_right = lax.ppermute(left, "col", [(z + 1, z) for z in range(n_col - 1)])
    tile = 256 if wide else 128
    weight_grad = pl.pallas_call(
        functools.partial(outer, tile),
        out_shape=jax.ShapeDtypeStruct((ff, d), f32),
        in_specs=[whole] * 2,
        out_specs=anywhere,
        scratch_shapes=[
            pltpu.VMEM((ff, d), f32),
            dma((ff // tile,)),
        ],
        compiler_params=pltpu.CompilerParams(vmem_limit_bytes=48 << 20),
        cost_estimate=pl.CostEstimate(
            flops=6 * tokens * ff * d, bytes_accessed=4 * ff * d, transcendentals=0
        ),
        name="outer",
    )(h_parts, g_parts)
    return weight_grad, own + (from_left + from_right)


def solution(mesh):
    placed = (P(("dp", "row"), "col"), P(("dp", "col"), "row"), P("row", "col"))
    return jax.shard_map(
        functools.partial(on_device, mesh.shape["row"], mesh.shape["col"]),
        mesh=mesh,
        in_specs=placed,
        out_specs=(P(("dp", "row"), "col"), P(("dp", "col"), "row")),
        check_vma=False,
    )
```
